32 devices in a mesh: dp: 16 (over z, y, core), tensor: 2 (over x).
Axes of the slice: x: 2, y: 2, z: 4, core: 2. Of those that a mesh axis runs over, the one named last changes fastest.
Arguments:
- layer_input: bfloat16 [10240, 1024], P('dp'), may hold values from -8 to 8
- output_grad: bfloat16 [10240, 1024], P('dp'), may hold values from -6 to 6
- attn_gain: float32 [1024], replicated, may hold values from 0.5 to 1.5
- attn_shift: float32 [1024], replicated, may hold values from -3 to 3
- mlp_gain: float32 [1024], replicated, may hold values from 0.5 to 1.5
- mlp_shift: float32 [1024], replicated, may hold values from -3 to 3
- qkv_weight: bfloat16 [1024, 3072], P(None, 'tensor'), may hold values from -1 to 1
- qkv_bias: float32 [3072], P('tensor'), may hold values from -3 to 3
- dense_weight: bfloat16 [1024, 1024], P('tensor'), may hold values from -0.75 to 0.75
- dense_bias: float32 [1024], replicated, may hold values from -3 to 3
- expand_weight: bfloat16 [1024, 4096], P(None, 'tensor'), may hold values from -0.1875 to 0.1875
- expand_bias: float32 [4096], P('tensor'), may hold values from -3 to 3
- contract_weight: bfloat16 [4096, 1024], P('tensor'), may hold values from -0.09375 to 0.09375
- contract_bias: float32 [1024], replicated, may hold values from -3 to 3
Outputs:
- layer_output: bfloat16 [10240, 1024], P('dp')
- input_grad: bfloat16 [10240, 1024], P('dp')
- attn_gain_grad: float32 [1024], replicated
- attn_shift_grad: float32 [1024], replicated
- mlp_gain_grad: float32 [1024], replicated
- mlp_shift_grad: float32 [1024], replicated
- qkv_weight_grad: float32 [1024, 3072], P('dp', 'tensor')
- qkv_bias_grad: float32 [3072], P('tensor')
- dense_weight_grad: float32 [1024, 1024], P('tensor', 'dp')
- dense_bias_grad: float32 [1024], replicated
- expand_weight_grad: float32 [1024, 4096], P('dp', 'tensor')
- expand_bias_grad: float32 [4096], P('tensor')
- contract_weight_grad: float32 [4096, 1024], P('tensor', 'dp')
- contract_bias_grad: float32 [1024], replicated
The draws below stay inside these ranges and needn't reach their ends.
All inputs are finite; a program needn't handle non-finite values.
Results may differ from the reference program's by a relative error of at most 0.0085.
The reference program's roundings to bfloat16 on the way (of `probs_low`, `context`, `active`, `hidden_low`, `context_grad`, `score_grad` and `mixed_low`) count: a program that leaves them out, or rounds other values in their place, can miss the bound.
Values sent between devices are 32-bit elements; how exact they have to be, the bound alone decides.
A program may use at most 192 MiB of HBM per device.

```python
import jax
import jax.numpy as jnp
from jax import lax

D = 1024
HEAD_DIM = 64
FF = 4096
ROT = 16
LEN = 640
TOKENS = 10240


def draw_layer_input(key, part):
    base = jax.random.normal(jax.random.fold_in(key, 1), (TOKENS, D), jnp.float32)
    return jnp.clip(base, -8.0, 8.0).astype(jnp.bfloat16)


def draw_qkv_weight(key, part):
    limit = 6.0 * D ** (-0.5)
    base = jax.random.normal(jax.random.fold_in(key, 11), (D, 3 * D), jnp.float32) * D ** (-0.5)
    base = jnp.clip(base, -limit, limit)
    return base.astype(jnp.bfloat16)


def block_scale(key, shape, cuts, least, largest):
    level = 1.0
    for position, blocks in cuts:
        steps = jax.random.uniform(jax.random.fold_in(jax.random.fold_in(key, 6), position), (blocks,), jnp.float32, least / len(cuts), largest / len(cuts))
        level = level * jnp.repeat(jnp.exp(steps), shape[position] // blocks).reshape((-1,) + (1,) * (len(shape) - 1 - position))
    return level


def gaussian(own_key, dims, deviation, bound, pieces=(), kind=jnp.bfloat16):
    array = deviation * jax.random.normal(own_key, dims, jnp.float32)
    if pieces:
        array = array * block_scale(own_key, dims, pieces, -0.22, 0.18)
    return jnp.clip(array, -bound, bound).astype(kind)


def setup_inputs(seed: int = 0) -> dict:
    seeds = jax.random.split(jax.random.key(seed), 15)
    layer_input = draw_layer_input(jax.random.fold_in(seeds[14], 71), 0)
    output_grad = gaussian(seeds[1], (TOKENS, D), 1.0, 6.0, ((0, 16),))
    attn_gain = jnp.clip(1.0 + 0.1 * jax.random.normal(seeds[2], (D,), jnp.float32), 0.5, 1.5)
    attn_shift = gaussian(seeds[3], (D,), 0.5, 3.0, (), jnp.float32)
    mlp_gain = jnp.clip(1.0 + 0.1 * jax.random.normal(seeds[4], (D,), jnp.float32), 0.5, 1.5)
    mlp_shift = gaussian(seeds[5], (D,), 0.5, 3.0, (), jnp.float32)
    qkv_weight = draw_qkv_weight(jax.random.fold_in(seeds[14], 71), 0)
    qkv_bias = gaussian(seeds[7], (3 * D,), 0.5, 3.0, ((0, 2),), jnp.float32)
    dense_weight = gaussian(seeds[8], (D, D), (D // 16) ** -0.5, 0.75, ((0, 2),))
    dense_bias = gaussian(seeds[9], (D,), 0.5, 3.0, (), jnp.float32)
    expand_weight = gaussian(seeds[10], (D, FF), D ** -0.5, 0.1875, ((1, 2),))
    expand_bias = gaussian(seeds[11], (FF,), 0.5, 3.0, ((0, 2),), jnp.float32)
    contract_weight = gaussian(seeds[12], (FF, D), FF ** -0.5, 0.09375, ((0, 2),))
    contract_bias = gaussian(seeds[13], (D,), 0.5, 3.0, (), jnp.float32)
    return {"layer_input": layer_input, "output_grad": output_grad, "attn_gain": attn_gain, "attn_shift": attn_shift, "mlp_gain": mlp_gain, "mlp_shift": mlp_shift, "qkv_weight": qkv_weight, "qkv_bias": qkv_bias, "dense_weight": dense_weight, "dense_bias": dense_bias, "expand_weight": expand_weight, "expand_bias": expand_bias, "contract_weight": contract_weight, "contract_bias": contract_bias}


NORM_EPS = 1e-05
SQRT_HALF = 0.7071067811865476
INV_ROOT_TWO_PI = 0.3989422804014327

def normalize(values):
    center = values - lax.optimization_barrier(jnp.mean(values, axis=1, keepdims=True))
    inverse = lax.rsqrt(lax.optimization_barrier(jnp.mean(center * center, axis=1, keepdims=True)) + NORM_EPS)
    return (center * inverse, inverse)

def norm_backward(norm_grad, scaling, unit_rows, inverse):
    scaled = norm_grad * scaling
    return inverse * (scaled - lax.optimization_barrier(jnp.mean(scaled, axis=1, keepdims=True)) - unit_rows * lax.optimization_barrier(jnp.mean(scaled * unit_rows, axis=1, keepdims=True)))

def rotary_tables(length):
    halfway = ROT // 2
    frequency = 10000.0 ** (-2.0 * jnp.arange(halfway, dtype=jnp.float32) / ROT)
    angles = jnp.arange(length, dtype=jnp.float32)[:, None] * frequency[None, :]
    return (jnp.cos(angles)[:, None, :], jnp.sin(angles)[:, None, :])

def rotate(vectors, cosine, sine_table, direction):
    halfway = ROT // 2
    first_half = vectors[..., :halfway]
    second_half = vectors[..., halfway:ROT]
    return jnp.concatenate([first_half * cosine - direction * second_half * sine_table, second_half * cosine + direction * first_half * sine_table, vectors[..., ROT:]], axis=-1)

def gelu_value(hidden_in):
    return 0.5 * hidden_in * (1.0 + lax.erf(hidden_in * SQRT_HALF))

def gelu_slope(hidden_in):
    return 0.5 * (1.0 + lax.erf(hidden_in * SQRT_HALF)) + hidden_in * jnp.exp(-0.5 * hidden_in * hidden_in) * INV_ROOT_TWO_PI

def sequence_pass(inputs, upstream, attn_gain, attn_shift, mlp_gain, mlp_shift, qkv_weight, qkv_bias, dense_weight, dense_bias, expand_weight, expand_bias, contract_weight, contract_bias):
    length = inputs.shape[0]
    heads_here = qkv_weight.shape[1] // (3 * HEAD_DIM)
    wide_input = inputs.astype(jnp.float32)
    unit_rows, inverse = normalize(wide_input)
    ln_attn = (unit_rows * attn_gain + attn_shift).astype(jnp.bfloat16)
    ln_mlp = (unit_rows * mlp_gain + mlp_shift).astype(jnp.bfloat16)
    cosine, sine_table = rotary_tables(length)
    mixed = (jnp.dot(ln_attn, qkv_weight, preferred_element_type=jnp.float32) + qkv_bias).reshape(length, heads_here, 3, HEAD_DIM)
    queries = rotate(mixed[:, :, 0], cosine, sine_table, 1.0).astype(jnp.bfloat16)
    keys_rot = rotate(mixed[:, :, 1], cosine, sine_table, 1.0).astype(jnp.bfloat16)
    values_low = mixed[:, :, 2].astype(jnp.bfloat16)
    causal = jnp.arange(length)[:, None] >= jnp.arange(length)[None, :]
    scores = jnp.einsum('qhd,khd->hqk', queries.astype(jnp.float32), keys_rot.astype(jnp.float32)) * HEAD_DIM ** (-0.5)
    scores = jnp.where(causal[None], scores, -jnp.inf)
    row_max = lax.optimization_barrier(jnp.max(scores, axis=2, keepdims=True))
    log_total = row_max + jnp.log(lax.optimization_barrier(jnp.sum(jnp.exp(scores - row_max), axis=2, keepdims=True)))
    probs = jnp.exp(scores - log_total)
    probs_low = probs.astype(jnp.bfloat16)
    context = jnp.einsum('hqk,khd->qhd', probs_low.astype(jnp.float32), values_low.astype(jnp.float32))
    context = context.astype(jnp.bfloat16).reshape(length, heads_here * HEAD_DIM)
    hidden = jnp.dot(ln_mlp, expand_weight, preferred_element_type=jnp.float32) + expand_bias
    active = gelu_value(hidden).astype(jnp.bfloat16)
    attn_part = jnp.dot(context, dense_weight, preferred_element_type=jnp.float32)
    mlp_part = jnp.dot(active, contract_weight, preferred_element_type=jnp.float32)
    layer_output = (wide_input + attn_part + mlp_part + dense_bias + contract_bias).astype(jnp.bfloat16)
    upstream_f = upstream.astype(jnp.float32)
    bias_term = lax.optimization_barrier(jnp.sum(upstream_f, axis=0))
    contract_term = jnp.dot(active.T, upstream, preferred_element_type=jnp.float32)
    dense_term = jnp.dot(context.T, upstream, preferred_element_type=jnp.float32)
    hidden_grad = jnp.dot(upstream, contract_weight.T, preferred_element_type=jnp.float32) * gelu_slope(hidden)
    expand_bias_term = lax.optimization_barrier(jnp.sum(hidden_grad, axis=0))
    hidden_low = hidden_grad.astype(jnp.bfloat16)
    expand_term = jnp.dot(ln_mlp.T, hidden_low, preferred_element_type=jnp.float32)
    mlp_norm_grad = jnp.dot(hidden_low, expand_weight.T, preferred_element_type=jnp.float32)
    context_grad = jnp.dot(upstream, dense_weight.T, preferred_element_type=jnp.float32)
    context_grad = context_grad.astype(jnp.bfloat16).reshape(length, heads_here, HEAD_DIM)
    value_grad = jnp.einsum('hqk,qhd->khd', probs_low.astype(jnp.float32), context_grad.astype(jnp.float32))
    prob_grad = jnp.einsum('qhd,khd->hqk', context_grad.astype(jnp.float32), values_low.astype(jnp.float32))
    row_delta = lax.optimization_barrier(jnp.sum(probs * prob_grad, axis=2, keepdims=True))
    score_grad = (probs * (prob_grad - row_delta) * HEAD_DIM ** (-0.5)).astype(jnp.bfloat16)
    query_grad = jnp.einsum('hqk,khd->qhd', score_grad.astype(jnp.float32), keys_rot.astype(jnp.float32))
    key_grad = jnp.einsum('hqk,qhd->khd', score_grad.astype(jnp.float32), queries.astype(jnp.float32))
    query_grad = rotate(query_grad, cosine, sine_table, -1.0)
    key_grad = rotate(key_grad, cosine, sine_table, -1.0)
    mixed_grad = jnp.stack([query_grad, key_grad, value_grad], axis=2).reshape(length, 3 * heads_here * HEAD_DIM)
    qkv_bias_term = lax.optimization_barrier(jnp.sum(mixed_grad, axis=0))
    mixed_low = mixed_grad.astype(jnp.bfloat16)
    qkv_term = jnp.dot(ln_attn.T, mixed_low, preferred_element_type=jnp.float32)
    attn_norm_grad = jnp.dot(mixed_low, qkv_weight.T, preferred_element_type=jnp.float32)
    attn_gain_term = lax.optimization_barrier(jnp.sum(attn_norm_grad * unit_rows, axis=0))
    attn_shift_term = lax.optimization_barrier(jnp.sum(attn_norm_grad, axis=0))
    mlp_gain_term = lax.optimization_barrier(jnp.sum(mlp_norm_grad * unit_rows, axis=0))
    mlp_shift_term = lax.optimization_barrier(jnp.sum(mlp_norm_grad, axis=0))
    input_grad = upstream_f + norm_backward(attn_norm_grad, attn_gain, unit_rows, inverse) + norm_backward(mlp_norm_grad, mlp_gain, unit_rows, inverse)
    input_grad = input_grad.astype(jnp.bfloat16)
    grads = (attn_gain_term, attn_shift_term, mlp_gain_term, mlp_shift_term, qkv_term, qkv_bias_term, dense_term, bias_term, expand_term, expand_bias_term, contract_term, bias_term)
    return (layer_output, input_grad, grads)

def reference(layer_input, output_grad, attn_gain, attn_shift, mlp_gain, mlp_shift, qkv_weight, qkv_bias, dense_weight, dense_bias, expand_weight, expand_bias, contract_weight, contract_bias):
    input_blocks = layer_input.reshape(-1, LEN, D)
    grad_blocks = output_grad.reshape(-1, LEN, D)
    shapes = (attn_gain, attn_shift, mlp_gain, mlp_shift, qkv_weight, qkv_bias, dense_weight, dense_bias, expand_weight, expand_bias, contract_weight, contract_bias)
    initial = tuple((jnp.zeros(param.shape, jnp.float32) for param in shapes))

    def step_fn(carry, pair):
        block_out, block_grad, grads = sequence_pass(pair[0], pair[1], attn_gain, attn_shift, mlp_gain, mlp_shift, qkv_weight, qkv_bias, dense_weight, dense_bias, expand_weight, expand_bias, contract_weight, contract_bias)
        carry = tuple((total + term for total, term in zip(carry, grads)))
        return (carry, (block_out, block_grad))
    totals, (outputs, input_grads) = lax.scan(step_fn, initial, (input_blocks, grad_blocks))
    layer_output = outputs.reshape(-1, D)
    input_grad = input_grads.reshape(-1, D)
    return (layer_output, input_grad, totals[0], totals[1], totals[2], totals[3], totals[4], totals[5], totals[6], totals[7], totals[8], totals[9], totals[10], totals[11])
```

```python
import functools

import jax
import jax.numpy as jnp
from jax import lax
from jax.experimental import pallas as pl
from jax.experimental.pallas import tpu as pltpu
from jax.sharding import PartitionSpec as P

HEAD_DIM = 64
ROT = 16


NORM_EPS = 1e-05
SQRT_HALF = 0.7071067811865476
INV_ROOT_TWO_PI = 0.3989422804014327


def normalize(values):
    center = values - jnp.mean(values, axis=1, keepdims=True)
    inverse = lax.rsqrt(jnp.mean(center * center, axis=1, keepdims=True) + NORM_EPS)
    return (center * inverse, inverse)


def rotary_tables(length):
    halfway = ROT // 2
    frequency = 10000.0 ** (-2.0 * jnp.arange(halfway, dtype=jnp.float32) / ROT)
    angles = jnp.arange(length, dtype=jnp.float32)[:, None] * frequency[None, :]
    cosine, sine = jnp.cos(angles), jnp.sin(angles)
    zeros = jnp.zeros((length, halfway), jnp.float32)
    rest_ones = jnp.ones((length, HEAD_DIM - ROT), jnp.float32)
    rest_zeros = jnp.zeros((length, HEAD_DIM - ROT), jnp.float32)
    whole = jnp.ones((length, HEAD_DIM), jnp.float32)
    blank = jnp.zeros((length, HEAD_DIM), jnp.float32)
    keep = jnp.concatenate([cosine, cosine, rest_ones], axis=1)
    ahead = jnp.concatenate([-sine, zeros, rest_zeros], axis=1)
    behind = jnp.concatenate([zeros, sine, rest_zeros], axis=1)
    return (
        jnp.concatenate([keep, keep, whole] * 2, axis=1),
        jnp.concatenate([ahead, ahead, blank] * 2, axis=1),
        jnp.concatenate([behind, behind, blank] * 2, axis=1),
    )


def gelu_value(hidden_in):
    return 0.5 * hidden_in * (1.0 + lax.erf(hidden_in * SQRT_HALF))


def gelu_slope(hidden_in):
    return (
        0.5 * (1.0 + lax.erf(hidden_in * SQRT_HALF))
        + hidden_in * jnp.exp(-0.5 * hidden_in * hidden_in) * INV_ROOT_TWO_PI
    )


def column_products(left_cols, right_rows):
    return lax.dot_general(
        left_cols, right_rows, (((0,), (0,)), ((), ())), preferred_element_type=jnp.float32
    )


NT = (((1,), (1,)), ((), ()))
TN = (((0,), (0,)), ((), ()))
PAIR = 6 * HEAD_DIM
LANES = 128


def dot32(left, right, dims=(((1,), (0,)), ((), ()))):
    return lax.dot_general(left, right, dims, preferred_element_type=jnp.float32)


def attention_kernel(
    ln_ref,
    up_ref,
    weight_ref,
    bias_ref,
    dense_ref,
    keep_ref,
    ahead_ref,
    behind_ref,
    context_ref,
    mixed_low_ref,
    bias_grad_ref,
    qkv_s,
    context_grad_s,
    grad_s,
):
    length = ln_ref.shape[0]
    block = LANES if length % LANES == 0 else length
    scale = HEAD_DIM ** (-0.5)
    mixed = dot32(ln_ref[...], weight_ref[...]) + bias_ref[...]
    for tile in range(PAIR // LANES):
        lanes = slice(tile * LANES, (tile + 1) * LANES)
        x = mixed[:, lanes]
        turned = (
            x * keep_ref[:, lanes]
            + pltpu.roll(x, LANES - ROT // 2, 1) * ahead_ref[:, lanes]
            + pltpu.roll(x, ROT // 2, 1) * behind_ref[:, lanes]
        )
        qkv_s[:, lanes] = turned.astype(jnp.bfloat16)
    context_grad_s[...] = dot32(up_ref[...], dense_ref[...], NT).astype(jnp.bfloat16)
    grad_s[...] = jnp.zeros_like(grad_s)
    for head in range(2):
        at = 3 * HEAD_DIM * head
        q_cols = slice(at, at + HEAD_DIM)
        k_cols = slice(at + HEAD_DIM, at + 2 * HEAD_DIM)
        v_cols = slice(at + 2 * HEAD_DIM, at + 3 * HEAD_DIM)
        own = slice(head * HEAD_DIM, (head + 1) * HEAD_DIM)
        for first in range(0, length, block):
            end = first + block
            rows = slice(first, end)
            q = qkv_s[rows, q_cols]
            k = qkv_s[:end, k_cols]
            v = qkv_s[:end, v_cols]
            context_grad = context_grad_s[rows, own]
            scores = dot32(q, k, NT) * scale
            row = lax.broadcasted_iota(jnp.int32, (block, end), 0) + first
            col = lax.broadcasted_iota(jnp.int32, (block, end), 1)
            scores = jnp.where(row >= col, scores, -jnp.inf)
            powers = jnp.exp(scores - jnp.max(scores, axis=1, keepdims=True))
            probs = powers * (1.0 / jnp.sum(powers, axis=1, keepdims=True))
            probs_low = probs.astype(jnp.bfloat16)
            context_ref[rows, own] = dot32(probs_low, v).astype(jnp.bfloat16)
            prob_grad = dot32(context_grad, v, NT)
            delta = jnp.sum(probs * prob_grad, axis=1, keepdims=True)
            score_grad = (probs * (prob_grad - delta) * scale).astype(jnp.bfloat16)
            grad_s[rows, q_cols] = dot32(score_grad, k)
            grad_s[:end, k_cols] += dot32(score_grad, q, TN)
            grad_s[:end, v_cols] += dot32(probs_low, context_grad, TN)
    for tile in range(PAIR // LANES):
        lanes = slice(tile * LANES, (tile + 1) * LANES)
        x = grad_s[:, lanes]
        back = (
            x * keep_ref[:, lanes]
            - pltpu.roll(x, LANES - ROT // 2, 1) * ahead_ref[:, lanes]
            - pltpu.roll(x, ROT // 2, 1) * behind_ref[:, lanes]
        )
        bias_grad_ref[:, lanes] = jnp.sum(back, axis=0, keepdims=True)
        mixed_low_ref[:, lanes] = back.astype(jnp.bfloat16)


def attention(ln_attn, upstream, qkv_weight, qkv_bias, dense_weight):
    length, width = ln_attn.shape
    qkv_cols = qkv_weight.shape[1]
    pairs = qkv_cols // PAIR
    tables = rotary_tables(length)
    whole = lambda p: (0, 0)
    across = lambda p: (0, p)
    return pl.pallas_call(
        attention_kernel,
        grid=(pairs,),
        in_specs=[
            pl.BlockSpec((length, width), whole),
            pl.BlockSpec((length, width), whole),
            pl.BlockSpec((width, PAIR), across),
            pl.BlockSpec((1, PAIR), across),
            pl.BlockSpec((2 * HEAD_DIM, width), lambda p: (p, 0)),
            pl.BlockSpec((length, PAIR), whole),
            pl.BlockSpec((length, PAIR), whole),
            pl.BlockSpec((length, PAIR), whole),
        ],
        out_specs=[
            pl.BlockSpec((length, 2 * HEAD_DIM), across),
            pl.BlockSpec((length, PAIR), across),
            pl.BlockSpec((1, PAIR), across),
        ],
        out_shape=[
            jax.ShapeDtypeStruct((length, pairs * 2 * HEAD_DIM), jnp.bfloat16),
            jax.ShapeDtypeStruct((length, qkv_cols), jnp.bfloat16),
            jax.ShapeDtypeStruct((1, qkv_cols), jnp.float32),
        ],
        scratch_shapes=[
            pltpu.VMEM((length, PAIR), jnp.bfloat16),
            pltpu.VMEM((length, 2 * HEAD_DIM), jnp.bfloat16),
            pltpu.VMEM((length, PAIR), jnp.float32),
        ],
        compiler_params=pltpu.CompilerParams(vmem_limit_bytes=40 * 1024 * 1024),
        cost_estimate=pl.CostEstimate(
            flops=2 * length * width * qkv_cols * 6,
            bytes_accessed=16 * 1024 * 1024,
            transcendentals=0,
        ),
    )(ln_attn, upstream, qkv_weight, qkv_bias.reshape(1, qkv_cols), dense_weight, *tables)


def tensor_sum(part, shards):
    if shards == 2:
        return part + lax.ppermute(part, "tensor", [(0, 1), (1, 0)])
    return lax.psum(part, "tensor")


def scatter_sum(term):
    return lax.psum_scatter(term, "dp", scatter_dimension=0, tiled=True)


def body(
    shards,
    layer_input,
    output_grad,
    attn_gain,
    attn_shift,
    mlp_gain,
    mlp_shift,
    qkv_weight,
    qkv_bias,
    dense_weight,
    dense_bias,
    expand_weight,
    expand_bias,
    contract_weight,
    contract_bias,
):
    qkv_cols = qkv_weight.shape[1]
    ff_here = expand_weight.shape[1]
    width = layer_input.shape[1]
    wide_input = layer_input.astype(jnp.float32)
    unit_rows, inverse = normalize(wide_input)
    ln_attn = (unit_rows * attn_gain + attn_shift).astype(jnp.bfloat16)
    ln_mlp = (unit_rows * mlp_gain + mlp_shift).astype(jnp.bfloat16)
    context, mixed_low, qkv_bias_term = attention(
        ln_attn, output_grad, qkv_weight, qkv_bias, dense_weight
    )
    hidden = dot32(ln_mlp, expand_weight) + expand_bias
    active = gelu_value(hidden).astype(jnp.bfloat16)
    partial_out = dot32(context, dense_weight) + dot32(active, contract_weight)
    branches = tensor_sum(partial_out, shards)
    layer_output = (wide_input + branches + dense_bias + contract_bias).astype(jnp.bfloat16)
    upstream_f = output_grad.astype(jnp.float32)
    active, hidden, mixed_low, _ = lax.optimization_barrier(
        (active, hidden, mixed_low, partial_out)
    )
    contract_summed = scatter_sum(column_products(output_grad, active))
    hidden_grad = dot32(output_grad, contract_weight, NT) * gelu_slope(hidden)
    expand_bias_term = jnp.sum(hidden_grad, axis=0)
    hidden_low = hidden_grad.astype(jnp.bfloat16)
    mlp_norm_part = dot32(hidden_low, expand_weight, NT)
    attn_norm_part = dot32(mixed_low, qkv_weight, NT)
    scaled_part = attn_norm_part * attn_gain + mlp_norm_part * mlp_gain
    scaled = tensor_sum(scaled_part, shards)
    hidden_low, mixed_low, context, _ = lax.optimization_barrier(
        (hidden_low, mixed_low, context, scaled_part)
    )
    expand_summed = scatter_sum(column_products(ln_mlp, hidden_low))
    qkv_summed = scatter_sum(column_products(ln_attn, mixed_low))
    dense_summed = scatter_sum(column_products(output_grad, context))
    me = lax.axis_index("tensor")
    slots = jnp.arange(shards)[:, None] == me
    small = jnp.concatenate(
        [
            jnp.sum(attn_norm_part * unit_rows, axis=0),
            jnp.sum(attn_norm_part, axis=0),
            jnp.sum(mlp_norm_part * unit_rows, axis=0),
            jnp.sum(mlp_norm_part, axis=0),
            jnp.where(me == 0, jnp.sum(upstream_f, axis=0), 0.0),
            jnp.where(slots, qkv_bias_term, 0.0).reshape(-1),
            jnp.where(slots, expand_bias_term[None], 0.0).reshape(-1),
        ]
    )
    small = lax.psum(small, ("dp", "tensor"))
    vectors = small[: 5 * width].reshape(5, width)
    qkv_bias_grad = lax.dynamic_slice(small, (5 * width + me * qkv_cols,), (qkv_cols,))
    expand_bias_grad = lax.dynamic_slice(
        small, (5 * width + shards * qkv_cols + me * ff_here,), (ff_here,)
    )
    input_back = inverse * (
        scaled
        - jnp.mean(scaled, axis=1, keepdims=True)
        - unit_rows * jnp.mean(scaled * unit_rows, axis=1, keepdims=True)
    )
    input_grad = (upstream_f + input_back).astype(jnp.bfloat16)
    return (
        layer_output,
        input_grad,
        vectors[0],
        vectors[1],
        vectors[2],
        vectors[3],
        qkv_summed,
        qkv_bias_grad,
        dense_summed.T,
        vectors[4],
        expand_summed,
        expand_bias_grad,
        contract_summed.T,
        vectors[4],
    )


def solution(mesh):
    in_specs = (
        P("dp", None),
        P("dp", None),
        P(),
        P(),
        P(),
        P(),
        P(None, "tensor"),
        P("tensor"),
        P("tensor", None),
        P(),
        P(None, "tensor"),
        P("tensor"),
        P("tensor", None),
        P(),
    )
    out_specs = (
        P("dp", None),
        P("dp", None),
        P(),
        P(),
        P(),
        P(),
        P("dp", "tensor"),
        P("tensor"),
        P("tensor", "dp"),
        P(),
        P("dp", "tensor"),
        P("tensor"),
        P("tensor", "dp"),
        P(),
    )
    return jax.shard_map(
        functools.partial(body, mesh.shape["tensor"]),
        mesh=mesh,
        in_specs=in_specs,
        out_specs=out_specs,
        check_vma=False,
    )
```

```python
import functools

import jax
import jax.numpy as jnp
import numpy as np
from jax import lax
from jax.experimental import pallas as pl
from jax.experimental.pallas import tpu as pltpu
from jax.sharding import PartitionSpec as P

HEAD_DIM = 64
ROT = 16


NORM_EPS = 1e-05
SQRT_HALF = 0.7071067811865476
INV_ROOT_TWO_PI = 0.3989422804014327


def normalize(values):
    center = values - jnp.mean(values, axis=1, keepdims=True)
    inverse = lax.rsqrt(jnp.mean(center * center, axis=1, keepdims=True) + NORM_EPS)
    return (center * inverse, inverse)


def rotary_tables(length):
    halfway = ROT // 2
    dim = lax.broadcasted_iota(jnp.int32, (length, LANES), 1) % HEAD_DIM
    position = lax.broadcasted_iota(jnp.int32, (length, LANES), 0).astype(jnp.float32)
    lane_dim = jnp.arange(LANES) % halfway
    frequency = 10000.0 ** (-2.0 * lane_dim.astype(jnp.float32) / ROT)
    angles = position * frequency[None, :]
    sine = jnp.sin(angles)
    keep = jnp.where(dim < ROT, jnp.cos(angles), 1.0)
    ahead = jnp.where(dim < halfway, -sine, 0.0)
    behind = jnp.where((dim >= halfway) & (dim < ROT), sine, 0.0)
    return keep, ahead, behind


def gelu_value(hidden_in):
    return 0.5 * hidden_in * (1.0 + lax.erf(hidden_in * SQRT_HALF))


def gelu_slope(hidden_in):
    return (
        0.5 * (1.0 + lax.erf(hidden_in * SQRT_HALF))
        + hidden_in * jnp.exp(-0.5 * hidden_in * hidden_in) * INV_ROOT_TWO_PI
    )


def column_products(left_cols, right_rows):
    return lax.dot_general(
        left_cols, right_rows, (((0,), (0,)), ((), ())), preferred_element_type=jnp.float32
    )


NT = (((1,), (1,)), ((), ()))
TN = (((0,), (0,)), ((), ()))
PAIR = 6 * HEAD_DIM
LANES = 128


def dot32(left, right, dims=(((1,), (0,)), ((), ()))):
    return lax.dot_general(left, right, dims, preferred_element_type=jnp.float32)


def attention_kernel(
    ln_ref,
    up_ref,
    weight_ref,
    bias_ref,
    dense_ref,
    keep_ref,
    ahead_ref,
    behind_ref,
    context_ref,
    mixed_low_ref,
    bias_grad_ref,
    qkv_s,
    context_grad_s,
    grad_s,
):
    length = ln_ref.shape[0]
    block = LANES if length % LANES == 0 else length
    scale = HEAD_DIM ** (-0.5)
    mixed = dot32(ln_ref[...], weight_ref[...]) + bias_ref[...]
    lane = lax.broadcasted_iota(jnp.int32, (length, LANES), 1)
    turned_lanes = (lane >= 0, lane >= HEAD_DIM, lane < HEAD_DIM)
    for tile in range(PAIR // LANES):
        lanes = slice(tile * LANES, (tile + 1) * LANES)
        x = mixed[:, lanes]
        turned = (
            x * keep_ref[...]
            + pltpu.roll(x, LANES - ROT // 2, 1) * ahead_ref[...]
            + pltpu.roll(x, ROT // 2, 1) * behind_ref[...]
        )
        qkv_s[:, lanes] = jnp.where(turned_lanes[tile], turned, x).astype(jnp.bfloat16)
    context_grad_s[...] = dot32(up_ref[...], dense_ref[...], NT).astype(jnp.bfloat16)
    grad_s[...] = jnp.zeros_like(grad_s)
    for head in range(2):
        at = 3 * HEAD_DIM * head
        q_cols = slice(at, at + HEAD_DIM)
        k_cols = slice(at + HEAD_DIM, at + 2 * HEAD_DIM)
        v_cols = slice(at + 2 * HEAD_DIM, at + 3 * HEAD_DIM)
        own = slice(head * HEAD_DIM, (head + 1) * HEAD_DIM)
        for first in range(0, length, block):
            end = first + block
            rows = slice(first, end)
            q = qkv_s[rows, q_cols]
            k = qkv_s[:end, k_cols]
            v = qkv_s[:end, v_cols]
            context_grad = context_grad_s[rows, own]
            scores = dot32(q, k, NT) * scale
            row = lax.broadcasted_iota(jnp.int32, (block, end), 0) + first
            col = lax.broadcasted_iota(jnp.int32, (block, end), 1)
            scores = jnp.where(row >= col, scores, -jnp.inf)
            powers = jnp.exp(scores - jnp.max(scores, axis=1, keepdims=True))
            probs = powers * (1.0 / jnp.sum(powers, axis=1, keepdims=True))
            probs_low = probs.astype(jnp.bfloat16)
            context_ref[rows, own] = dot32(probs_low, v).astype(jnp.bfloat16)
            prob_grad = dot32(context_grad, v, NT)
            delta = jnp.sum(probs * prob_grad, axis=1, keepdims=True)
            score_grad = (probs * (prob_grad - delta) * scale).astype(jnp.bfloat16)
            grad_s[rows, q_cols] = dot32(score_grad, k)
            grad_s[:end, k_cols] += dot32(score_grad, q, TN)
            grad_s[:end, v_cols] += dot32(probs_low, context_grad, TN)
    for tile in range(PAIR // LANES):
        lanes = slice(tile * LANES, (tile + 1) * LANES)
        x = grad_s[:, lanes]
        back = (
            x * keep_ref[...]
            - pltpu.roll(x, LANES - ROT // 2, 1) * ahead_ref[...]
            - pltpu.roll(x, ROT // 2, 1) * behind_ref[...]
        )
        back = jnp.where(turned_lanes[tile], back, x)
        bias_grad_ref[:, lanes] = jnp.sum(back, axis=0, keepdims=True)
        mixed_low_ref[:, lanes] = back.astype(jnp.bfloat16)


def attention(ln_attn, upstream, qkv_weight, qkv_bias, dense_weight):
    length, width = ln_attn.shape
    qkv_cols = qkv_weight.shape[1]
    pairs = qkv_cols // PAIR
    tables = rotary_tables(length)
    whole = lambda p: (0, 0)
    across = lambda p: (0, p)
    return pl.pallas_call(
        attention_kernel,
        grid=(pairs,),
        in_specs=[
            pl.BlockSpec((length, width), whole),
            pl.BlockSpec((length, width), whole),
            pl.BlockSpec((width, PAIR), across),
            pl.BlockSpec((1, PAIR), across),
            pl.BlockSpec((2 * HEAD_DIM, width), lambda p: (p, 0)),
            pl.BlockSpec((length, LANES), whole),
            pl.BlockSpec((length, LANES), whole),
            pl.BlockSpec((length, LANES), whole),
        ],
        out_specs=[
            pl.BlockSpec((length, 2 * HEAD_DIM), across),
            pl.BlockSpec((length, PAIR), across),
            pl.BlockSpec((1, PAIR), across),
        ],
        out_shape=[
            jax.ShapeDtypeStruct((length, pairs * 2 * HEAD_DIM), jnp.bfloat16),
            jax.ShapeDtypeStruct((length, qkv_cols), jnp.bfloat16),
            jax.ShapeDtypeStruct((1, qkv_cols), jnp.float32),
        ],
        scratch_shapes=[
            pltpu.VMEM((length, PAIR), jnp.bfloat16),
            pltpu.VMEM((length, 2 * HEAD_DIM), jnp.bfloat16),
            pltpu.VMEM((length, PAIR), jnp.float32),
        ],
        compiler_params=pltpu.CompilerParams(vmem_limit_bytes=40 * 1024 * 1024),
        cost_estimate=pl.CostEstimate(
            flops=2 * length * width * qkv_cols * 6,
            bytes_accessed=16 * 1024 * 1024,
            transcendentals=0,
        ),
    )(ln_attn, upstream, qkv_weight, qkv_bias.reshape(1, qkv_cols), dense_weight, *tables)


def swapped(array, axis, size, bit):
    return lax.ppermute(array, axis, [(i, i ^ bit) for i in range(size)])


def all_sum(part, axis, size, gate):
    bit = 1
    while bit < size:
        got = swapped(part, axis, size, bit)
        if gate is not None:
            got, _ = lax.optimization_barrier((got, gate))
        part = part + got
        bit *= 2
    return part


def owner_order(columns, size):
    bits = size.bit_length() - 1
    block = columns // size
    flips = np.array([int(f"{p:0{bits}b}"[::-1], 2) if bits else 0 for p in range(size)])
    owner = jnp.asarray(flips, jnp.int32) ^ lax.axis_index("dp")
    source = (owner[:, None] * block + jnp.arange(block)[None, :]).reshape(1, columns)
    return (jnp.arange(columns)[:, None] == source).astype(jnp.bfloat16)


def ordered(rows, order):
    return dot32(rows, order).astype(jnp.bfloat16)


def first_halving(left, right, size):
    half = left.shape[1] // 2
    return column_products(left[:, :half], right) + swapped(
        column_products(left[:, half:], right), "dp", size, 1
    )


def halving(part, size, bit):
    half = part.shape[0] // 2
    return part[:half] + swapped(part[half:], "dp", size, bit)


def halvings(part, size, bit):
    while bit < size:
        part = halving(part, size, bit)
        bit *= 2
    return part


def body(
    shards,
    replicas,
    layer_input,
    output_grad,
    attn_gain,
    attn_shift,
    mlp_gain,
    mlp_shift,
    qkv_weight,
    qkv_bias,
    dense_weight,
    dense_bias,
    expand_weight,
    expand_bias,
    contract_weight,
    contract_bias,
):
    qkv_cols = qkv_weight.shape[1]
    width = layer_input.shape[1]
    wide_input = layer_input.astype(jnp.float32)
    unit_rows, inverse = normalize(wide_input)
    ln_attn = (unit_rows * attn_gain + attn_shift).astype(jnp.bfloat16)
    ln_mlp = (unit_rows * mlp_gain + mlp_shift).astype(jnp.bfloat16)
    context, mixed_low, qkv_bias_term = attention(
        ln_attn, output_grad, qkv_weight, qkv_bias, dense_weight
    )
    hidden = dot32(ln_mlp, expand_weight) + expand_bias
    active = gelu_value(hidden).astype(jnp.bfloat16)
    partial_out = dot32(context, dense_weight) + dot32(active, contract_weight)
    upstream_f = output_grad.astype(jnp.float32)
    active, hidden, mixed_low, _ = lax.optimization_barrier(
        (active, hidden, mixed_low, partial_out)
    )
    order = owner_order(width, replicas)
    up_ordered = ordered(output_grad, order)
    contract_part = first_halving(up_ordered, active, replicas)
    hidden_grad = dot32(output_grad, contract_weight, NT) * gelu_slope(hidden)
    expand_bias_term = jnp.sum(hidden_grad, axis=0)
    hidden_low = hidden_grad.astype(jnp.bfloat16)
    mlp_norm_part = dot32(hidden_low, expand_weight, NT)
    attn_norm_part = dot32(mixed_low, qkv_weight, NT)
    scaled_part = attn_norm_part * attn_gain + mlp_norm_part * mlp_gain
    hidden_low, mixed_low, context, _ = lax.optimization_barrier(
        (hidden_low, mixed_low, context, scaled_part)
    )
    expand_part = first_halving(ordered(ln_mlp, order), hidden_low, replicas)
    qkv_part = first_halving(ordered(ln_attn, order), mixed_low, replicas)
    dense_part = first_halving(up_ordered, context, replicas)
    contract_half = halving(contract_part, replicas, 2)
    expand_half = halving(expand_part, replicas, 2)
    qkv_half = halving(qkv_part, replicas, 2)
    contract_quarter = halving(contract_half, replicas, 4) if replicas > 4 else contract_half
    contract_summed = halvings(contract_quarter, replicas, 8)
    expand_summed = halvings(expand_half, replicas, 4)
    qkv_summed = halvings(qkv_half, replicas, 4)
    dense_summed = halvings(dense_part, replicas, 2)
    branches = all_sum(partial_out, "tensor", shards, expand_half)
    layer_output = (wide_input + branches + dense_bias + contract_bias).astype(jnp.bfloat16)
    scaled = all_sum(scaled_part, "tensor", shards, contract_quarter)
    small = jnp.concatenate(
        [
            jnp.sum(attn_norm_part * unit_rows, axis=0),
            jnp.sum(attn_norm_part, axis=0),
            jnp.sum(mlp_norm_part * unit_rows, axis=0),
            jnp.sum(mlp_norm_part, axis=0),
            jnp.sum(upstream_f, axis=0),
            qkv_bias_term.reshape(-1),
            expand_bias_term,
        ]
    )
    small = all_sum(small, "dp", replicas, expand_half)
    vectors = all_sum(small[: 4 * width], "tensor", shards, None).reshape(4, width)
    bias_grad = small[4 * width : 5 * width]
    qkv_bias_grad = small[5 * width : 5 * width + qkv_cols]
    expand_bias_grad = small[5 * width + qkv_cols :]
    input_back = inverse * (
        scaled
        - jnp.mean(scaled, axis=1, keepdims=True)
        - unit_rows * jnp.mean(scaled * unit_rows, axis=1, keepdims=True)
    )
    input_grad = (upstream_f + input_back).astype(jnp.bfloat16)
    return (
        layer_output,
        input_grad,
        vectors[0],
        vectors[1],
        vectors[2],
        vectors[3],
        qkv_summed,
        qkv_bias_grad,
        dense_summed.T,
        bias_grad,
        expand_summed,
        expand_bias_grad,
        contract_summed.T,
        bias_grad,
    )


def solution(mesh):
    in_specs = (
        P("dp", None),
        P("dp", None),
        P(),
        P(),
        P(),
        P(),
        P(None, "tensor"),
        P("tensor"),
        P("tensor", None),
        P(),
        P(None, "tensor"),
        P("tensor"),
        P("tensor", None),
        P(),
    )
    out_specs = (
        P("dp", None),
        P("dp", None),
        P(),
        P(),
        P(),
        P(),
        P("dp", "tensor"),
        P("tensor"),
        P("tensor", "dp"),
        P(),
        P("dp", "tensor"),
        P("tensor"),
        P("tensor", "dp"),
        P(),
    )
    return jax.shard_map(
        functools.partial(body, mesh.shape["tensor"], mesh.shape["dp"]),
        mesh=mesh,
        in_specs=in_specs,
        out_specs=out_specs,
        check_vma=False,
    )
```

```python
import functools

import jax
import jax.numpy as jnp
import numpy as np
from jax import lax
from jax.experimental import pallas as pl
from jax.experimental.pallas import tpu as pltpu
from jax.sharding import PartitionSpec as P

HEAD_DIM = 64
ROT = 16


NORM_EPS = 1e-05
SQRT_HALF = 0.7071067811865476
INV_ROOT_TWO_PI = 0.3989422804014327


def normalize(values):
    center = values - jnp.mean(values, axis=1, keepdims=True)
    inverse = lax.rsqrt(jnp.mean(center * center, axis=1, keepdims=True) + NORM_EPS)
    return (center * inverse, inverse)


def rotary_tables(length):
    halfway = ROT // 2
    dim = lax.broadcasted_iota(jnp.int32, (length, LANES), 1) % HEAD_DIM
    position = lax.broadcasted_iota(jnp.int32, (length, LANES), 0).astype(jnp.float32)
    lane_dim = jnp.arange(LANES) % halfway
    frequency = 10000.0 ** (-2.0 * lane_dim.astype(jnp.float32) / ROT)
    angles = position * frequency[None, :]
    sine = jnp.sin(angles)
    keep = jnp.where(dim < ROT, jnp.cos(angles), 1.0)
    ahead = jnp.where(dim < halfway, -sine, 0.0)
    behind = jnp.where((dim >= halfway) & (dim < ROT), sine, 0.0)
    return keep, ahead, behind


def gelu_value(hidden_in):
    return 0.5 * hidden_in * (1.0 + lax.erf(hidden_in * SQRT_HALF))


def gelu_slope(hidden_in):
    return (
        0.5 * (1.0 + lax.erf(hidden_in * SQRT_HALF))
        + hidden_in * jnp.exp(-0.5 * hidden_in * hidden_in) * INV_ROOT_TWO_PI
    )


def column_products(left_cols, right_rows):
    return lax.dot_general(
        left_cols, right_rows, (((0,), (0,)), ((), ())), preferred_element_type=jnp.float32
    )


NT = (((1,), (1,)), ((), ()))
TN = (((0,), (0,)), ((), ()))
PAIR = 6 * HEAD_DIM
LANES = 128


def dot32(left, right, dims=(((1,), (0,)), ((), ()))):
    return lax.dot_general(left, right, dims, preferred_element_type=jnp.float32)


def attention_kernel(
    ln_ref,
    up_ref,
    weight_ref,
    bias_ref,
    dense_ref,
    keep_ref,
    ahead_ref,
    behind_ref,
    context_ref,
    mixed_low_ref,
    bias_grad_ref,
    qkv_s,
    context_grad_s,
    grad_s,
):
    length = ln_ref.shape[0]
    block = LANES if length % LANES == 0 else length
    scale = HEAD_DIM ** (-0.5)
    mixed = dot32(ln_ref[...], weight_ref[...]) + bias_ref[...]
    lane = lax.broadcasted_iota(jnp.int32, (length, LANES), 1)
    turned_lanes = (lane >= 0, lane >= HEAD_DIM, lane < HEAD_DIM)
    for tile in range(PAIR // LANES):
        lanes = slice(tile * LANES, (tile + 1) * LANES)
        x = mixed[:, lanes]
        turned = (
            x * keep_ref[...]
            + pltpu.roll(x, LANES - ROT // 2, 1) * ahead_ref[...]
            + pltpu.roll(x, ROT // 2, 1) * behind_ref[...]
        )
        qkv_s[:, lanes] = jnp.where(turned_lanes[tile], turned, x).astype(jnp.bfloat16)
    context_grad_s[...] = dot32(up_ref[...], dense_ref[...], NT).astype(jnp.bfloat16)
    grad_s[...] = jnp.zeros_like(grad_s)
    for head in range(2):
        at = 3 * HEAD_DIM * head
        q_cols = slice(at, at + HEAD_DIM)
        k_cols = slice(at + HEAD_DIM, at + 2 * HEAD_DIM)
        v_cols = slice(at + 2 * HEAD_DIM, at + 3 * HEAD_DIM)
        own = slice(head * HEAD_DIM, (head + 1) * HEAD_DIM)
        for first in range(0, length, block):
            end = first + block
            rows = slice(first, end)
            q = qkv_s[rows, q_cols]
            k = qkv_s[:end, k_cols]
            v = qkv_s[:end, v_cols]
            context_grad = context_grad_s[rows, own]
            scores = dot32(q, k, NT) * scale
            row = lax.broadcasted_iota(jnp.int32, (block, end), 0) + first
            col = lax.broadcasted_iota(jnp.int32, (block, end), 1)
            scores = jnp.where(row >= col, scores, -jnp.inf)
            powers = jnp.exp(scores - jnp.max(scores, axis=1, keepdims=True))
            probs = powers * (1.0 / jnp.sum(powers, axis=1, keepdims=True))
            probs_low = probs.astype(jnp.bfloat16)
            context_ref[rows, own] = dot32(probs_low, v).astype(jnp.bfloat16)
            prob_grad = dot32(context_grad, v, NT)
            delta = jnp.sum(probs * prob_grad, axis=1, keepdims=True)
            score_grad = (probs * (prob_grad - delta) * scale).astype(jnp.bfloat16)
            grad_s[rows, q_cols] = dot32(score_grad, k)
            grad_s[:end, k_cols] += dot32(score_grad, q, TN)
            grad_s[:end, v_cols] += dot32(probs_low, context_grad, TN)
    for tile in range(PAIR // LANES):
        lanes = slice(tile * LANES, (tile + 1) * LANES)
        x = grad_s[:, lanes]
        back = (
            x * keep_ref[...]
            - pltpu.roll(x, LANES - ROT // 2, 1) * ahead_ref[...]
            - pltpu.roll(x, ROT // 2, 1) * behind_ref[...]
        )
        back = jnp.where(turned_lanes[tile], back, x)
        bias_grad_ref[:, lanes] = jnp.sum(back, axis=0, keepdims=True)
        mixed_low_ref[:, lanes] = back.astype(jnp.bfloat16)


def attention(ln_attn, upstream, qkv_weight, qkv_bias, dense_weight):
    length, width = ln_attn.shape
    qkv_cols = qkv_weight.shape[1]
    pairs = qkv_cols // PAIR
    tables = rotary_tables(length)
    whole = lambda p: (0, 0)
    across = lambda p: (0, p)
    return pl.pallas_call(
        attention_kernel,
        grid=(pairs,),
        in_specs=[
            pl.BlockSpec((length, width), whole),
            pl.BlockSpec((length, width), whole),
            pl.BlockSpec((width, PAIR), across),
            pl.BlockSpec((1, PAIR), across),
            pl.BlockSpec((2 * HEAD_DIM, width), lambda p: (p, 0)),
            pl.BlockSpec((length, LANES), whole),
            pl.BlockSpec((length, LANES), whole),
            pl.BlockSpec((length, LANES), whole),
        ],
        out_specs=[
            pl.BlockSpec((length, 2 * HEAD_DIM), across),
            pl.BlockSpec((length, PAIR), across),
            pl.BlockSpec((1, PAIR), across),
        ],
        out_shape=[
            jax.ShapeDtypeStruct((length, pairs * 2 * HEAD_DIM), jnp.bfloat16),
            jax.ShapeDtypeStruct((length, qkv_cols), jnp.bfloat16),
            jax.ShapeDtypeStruct((1, qkv_cols), jnp.float32),
        ],
        scratch_shapes=[
            pltpu.VMEM((length, PAIR), jnp.bfloat16),
            pltpu.VMEM((length, 2 * HEAD_DIM), jnp.bfloat16),
            pltpu.VMEM((length, PAIR), jnp.float32),
        ],
        compiler_params=pltpu.CompilerParams(vmem_limit_bytes=40 * 1024 * 1024),
        cost_estimate=pl.CostEstimate(
            flops=2 * length * width * qkv_cols * 6,
            bytes_accessed=16 * 1024 * 1024,
            transcendentals=0,
        ),
    )(ln_attn, upstream, qkv_weight, qkv_bias.reshape(1, qkv_cols), dense_weight, *tables)


def swapped(array, axis, size, bit):
    return lax.ppermute(array, axis, [(i, i ^ bit) for i in range(size)])


def all_sum(part, axis, size, gate):
    bit = 1
    while bit < size:
        got = swapped(part, axis, size, bit)
        if gate is not None:
            got, _ = lax.optimization_barrier((got, gate))
        part = part + got
        bit *= 2
    return part


def owner_order(columns, size, bits):
    block = columns // size
    flips = np.zeros(size, np.int32)
    for stage, bit in enumerate(bits):
        flips ^= np.where(np.arange(size) >> (len(bits) - 1 - stage) & 1, bit, 0).astype(np.int32)
    owner = jnp.asarray(flips) ^ lax.axis_index("dp")
    source = (owner[:, None] * block + jnp.arange(block)[None, :]).reshape(1, columns)
    return (jnp.arange(columns)[:, None] == source).astype(jnp.bfloat16)


def ordered(rows, order):
    return dot32(rows, order).astype(jnp.bfloat16)


def first_halving(left, right, size):
    half = left.shape[1] // 2
    return column_products(left[:, :half], right) + swapped(
        column_products(left[:, half:], right), "dp", size, 1
    )


def halving(part, size, bit):
    half = part.shape[0] // 2
    return part[:half] + swapped(part[half:], "dp", size, bit)


def halvings(part, size, bits):
    for bit in bits:
        part = halving(part, size, bit)
    return part


def body(
    shards,
    replicas,
    layer_input,
    output_grad,
    attn_gain,
    attn_shift,
    mlp_gain,
    mlp_shift,
    qkv_weight,
    qkv_bias,
    dense_weight,
    dense_bias,
    expand_weight,
    expand_bias,
    contract_weight,
    contract_bias,
):
    qkv_cols = qkv_weight.shape[1]
    width = layer_input.shape[1]
    wide_input = layer_input.astype(jnp.float32)
    unit_rows, inverse = normalize(wide_input)
    ln_attn = (unit_rows * attn_gain + attn_shift).astype(jnp.bfloat16)
    ln_mlp = (unit_rows * mlp_gain + mlp_shift).astype(jnp.bfloat16)
    context, mixed_low, qkv_bias_term = attention(
        ln_attn, output_grad, qkv_weight, qkv_bias, dense_weight
    )
    hidden = dot32(ln_mlp, expand_weight) + expand_bias
    active = gelu_value(hidden).astype(jnp.bfloat16)
    partial_out = dot32(context, dense_weight) + dot32(active, contract_weight)
    upstream_f = output_grad.astype(jnp.float32)
    active, hidden, mixed_low, _ = lax.optimization_barrier(
        (active, hidden, mixed_low, partial_out)
    )
    bits = [1 << b for b in range(replicas.bit_length() - 1)]
    turned_bits = bits[:1] + bits[2:] + bits[1:2]
    order = owner_order(width, replicas, bits)
    turned_order = owner_order(width, replicas, turned_bits)
    up_ordered = ordered(output_grad, order)
    contract_part = first_halving(up_ordered, active, replicas)
    hidden_grad = dot32(output_grad, contract_weight, NT) * gelu_slope(hidden)
    expand_bias_term = jnp.sum(hidden_grad, axis=0)
    hidden_low = hidden_grad.astype(jnp.bfloat16)
    mlp_norm_part = dot32(hidden_low, expand_weight, NT)
    attn_norm_part = dot32(mixed_low, qkv_weight, NT)
    scaled_part = attn_norm_part * attn_gain + mlp_norm_part * mlp_gain
    hidden_low, mixed_low, context, _ = lax.optimization_barrier(
        (hidden_low, mixed_low, context, scaled_part)
    )
    expand_part = first_halving(ordered(ln_mlp, order), hidden_low, replicas)
    qkv_part = first_halving(ordered(ln_attn, turned_order), mixed_low, replicas)
    dense_part = first_halving(up_ordered, context, replicas)
    contract_half = halving(contract_part, replicas, 2)
    expand_half = halving(expand_part, replicas, 2)
    contract_quarter = halving(contract_half, replicas, 4)
    contract_summed = halvings(contract_quarter, replicas, bits[3:])
    expand_summed = halvings(expand_half, replicas, bits[2:])
    qkv_summed = halvings(qkv_part, replicas, turned_bits[1:])
    dense_summed = halvings(dense_part, replicas, bits[1:])
    branches = all_sum(partial_out, "tensor", shards, expand_half)
    layer_output = (wide_input + branches + dense_bias + contract_bias).astype(jnp.bfloat16)
    scaled = all_sum(scaled_part, "tensor", shards, contract_quarter)
    small = jnp.concatenate(
        [
            jnp.sum(attn_norm_part * unit_rows, axis=0),
            jnp.sum(attn_norm_part, axis=0),
            jnp.sum(mlp_norm_part * unit_rows, axis=0),
            jnp.sum(mlp_norm_part, axis=0),
            jnp.sum(upstream_f, axis=0),
            qkv_bias_term.reshape(-1),
            expand_bias_term,
        ]
    )
    small = all_sum(small, "dp", replicas, expand_half)
    vectors = all_sum(small[: 4 * width], "tensor", shards, None).reshape(4, width)
    bias_grad = small[4 * width : 5 * width]
    qkv_bias_grad = small[5 * width : 5 * width + qkv_cols]
    expand_bias_grad = small[5 * width + qkv_cols :]
    input_back = inverse * (
        scaled
        - jnp.mean(scaled, axis=1, keepdims=True)
        - unit_rows * jnp.mean(scaled * unit_rows, axis=1, keepdims=True)
    )
    input_grad = (upstream_f + input_back).astype(jnp.bfloat16)
    return (
        layer_output,
        input_grad,
        vectors[0],
        vectors[1],
        vectors[2],
        vectors[3],
        qkv_summed,
        qkv_bias_grad,
        dense_summed.T,
        bias_grad,
        expand_summed,
        expand_bias_grad,
        contract_summed.T,
        bias_grad,
    )


def solution(mesh):
    in_specs = (
        P("dp", None),
        P("dp", None),
        P(),
        P(),
        P(),
        P(),
        P(None, "tensor"),
        P("tensor"),
        P("tensor", None),
        P(),
        P(None, "tensor"),
        P("tensor"),
        P("tensor", None),
        P(),
    )
    out_specs = (
        P("dp", None),
        P("dp", None),
        P(),
        P(),
        P(),
        P(),
        P("dp", "tensor"),
        P("tensor"),
        P("tensor", "dp"),
        P(),
        P("dp", "tensor"),
        P("tensor"),
        P("tensor", "dp"),
        P(),
    )
    return jax.shard_map(
        functools.partial(body, mesh.shape["tensor"], mesh.shape["dp"]),
        mesh=mesh,
        in_specs=in_specs,
        out_specs=out_specs,
        check_vma=False,
    )
```
